32 devices in a mesh: ctx: 8 (over z, x), head: 4 (over y, core).
Axes of the slice: x: 2, y: 2, z: 4, core: 2. Of those that a mesh axis runs over, the one named last changes fastest.
Arguments:
- queries: bfloat16 [384, 5120], P('ctx', 'head'), as said below
- draft_keys: bfloat16 [384, 1024], P('ctx', 'head'), may hold values from -2.5 to 2.5
- draft_values: bfloat16 [384, 1024], P('ctx', 'head'), may hold values from -6 to 6
- cache_keys: bfloat16 [512, 128, 8, 128], P('ctx', None, 'head'), as said below
- cache_values: bfloat16 [512, 128, 8, 128], P('ctx', None, 'head'), may hold values from -6 to 6
- w_out: bfloat16 [5120, 5120], P('head', 'ctx'), may hold values from -0.078125 to 0.078125
- lengths: int32 [24], replicated, may hold values from 1 to 16384, as said below
- block_req: int32 [512], replicated, may hold values from 0 to 23, as said below
- block_idx: int32 [512], replicated, may hold values from -1 to 127
- move_dst: int32 [512], replicated, may hold values from -1 to 7, as said below
- draft_offs: int32 [24, 16], replicated, may hold values from 0 to 15, as said below
Outputs:
- mixed: bfloat16 [384, 5120], P('head', 'ctx')
- new_keys: bfloat16 [576, 128, 8, 128], P('ctx', None, 'head')
- new_values: bfloat16 [576, 128, 8, 128], P('ctx', None, 'head')
The draws below stay inside these ranges and needn't reach their ends.
Inputs may be any that keep to these rules, and one draw needn't show every extreme that they name: queries lie within -6 to 6. cache_keys lie within -6 to 6. Request r has exactly ceil(lengths[r] / 128) blocks, numbered from 0, each in exactly one slot. Empty slots hold block_req 0; on each index of ctx the live slots come before the empty ones. `move_dst`: only live blocks move, never to their own index; at most 2 blocks go from one index of ctx to one other and at most 8 arrive at one index, both reached. draft_offs[r, t] <= t.
All inputs are finite; a program needn't handle non-finite values.
Results may differ from the reference program's by a relative error of at most 0.0051.
Values may be sent and summed in bfloat16 or wider, within the bound.
A program may use at most 128 MiB of HBM per device.

```python
import math
import jax
import jax.numpy as jnp
from jax import lax

D = 5120
QH = 40
KVH = 8
HD = 128
GROUP = 5
DRAFT = 16
REQS = 24
BLK = 128
BLOCKS_DEV = 64
IN_DEV = 8
NBLK = 512
TOKENS = 384
N_CTX = 8


def draw_queries(key, part):
    values = jax.random.uniform(key, (TOKENS, QH * HD), jnp.float32, -6.0, 6.0)
    return values.astype(jnp.bfloat16)


def draw_cache_keys(key, part):
    values = jnp.clip(0.3 * jax.random.normal(key, (NBLK, BLK, KVH, HD), jnp.float32), -6.0, 6.0)
    return values.astype(jnp.bfloat16)


def plan_tables(key):
    base = jax.random.fold_in(key, 9173)
    keys = jax.random.split(base, 6)
    ndev = NBLK // BLOCKS_DEV
    half = ndev // 2
    devs = jnp.arange(ndev, dtype=jnp.int32)
    shuffled = jax.random.permutation(keys[0], ndev - 1).astype(jnp.int32)
    rank_of = jnp.full((ndev,), ndev - 1, jnp.int32).at[shuffled].set(jnp.arange(ndev - 1, dtype=jnp.int32))
    heavy = (rank_of < half).astype(jnp.int32)
    light = 1 - heavy
    receiver = jnp.sum(jnp.where(rank_of == half, devs, 0))
    low = jax.random.randint(keys[1], (ndev,), BLOCKS_DEV // 4, BLOCKS_DEV // 2 + 1).astype(jnp.int32)
    count = jnp.where(heavy == 1, BLOCKS_DEV, low).astype(jnp.int32)
    moves = jax.random.randint(keys[2], (ndev, ndev), 1, 3).astype(jnp.int32) * heavy[:, None] * light[None, :]
    moves = jnp.where((devs[None, :] == receiver) & (heavy[:, None] == 1), 2, moves).astype(jnp.int32)
    out_count = jnp.sum(moves, axis=1)
    cum = jnp.cumsum(moves, axis=1)
    slots = jnp.arange(BLOCKS_DEV, dtype=jnp.int32)
    offset = slots[None, :] - (count - out_count)[:, None]
    live = slots[None, :] < count[:, None]
    moved = (offset >= 0) & live
    dst = jnp.sum((cum[:, None, :] <= offset[:, :, None]).astype(jnp.int32), axis=2)
    move_dst = jnp.where(moved, dst, -1).astype(jnp.int32).reshape(-1)
    start_dev = jnp.cumsum(count) - count
    rank = start_dev[:, None] + slots[None, :]
    total = jnp.sum(count)
    longest = NBLK // 4
    reqs_line = jnp.arange(REQS, dtype=jnp.int32)
    long_id = jax.random.randint(keys[5], (), 0, REQS).astype(jnp.int32)
    is_long = reqs_line == long_id
    weights = jnp.where(is_long, 0, 1 + jax.random.randint(keys[3], (REQS,), 0, 2)).astype(jnp.int32)
    extra = total - longest - (REQS - 1)
    cum_in = jnp.cumsum(weights)
    cum_ex = cum_in - weights
    wsum = jnp.sum(weights)
    others = 1 + extra * cum_in // wsum - extra * cum_ex // wsum
    blocks_of = jnp.where(is_long, longest, others).astype(jnp.int32)
    start = jnp.cumsum(blocks_of) - blocks_of
    req = jnp.sum((start[None, None, :] <= rank[:, :, None]).astype(jnp.int32), axis=2) - 1
    req = jnp.clip(req, 0, REQS - 1)
    idx = rank - jnp.take(start, req)
    block_req = jnp.where(live, req, 0).astype(jnp.int32).reshape(-1)
    block_idx = jnp.where(live, idx, -1).astype(jnp.int32).reshape(-1)
    trim = jnp.where(is_long, 0, jax.random.randint(keys[4], (REQS,), 0, BLK - 1))
    lengths = (blocks_of * BLK - trim).astype(jnp.int32)
    return (lengths, block_req, block_idx, move_dst)


def draw_lengths(key, part):
    return plan_tables(key)[0]


def draw_block_req(key, part):
    return plan_tables(key)[1]


def draw_block_idx(key, part):
    return plan_tables(key)[2]


def draw_move_dst(key, part):
    return plan_tables(key)[3]


def draw_draft_offs(key, part):
    base = jax.random.fold_in(key, 3307)
    tpos = jnp.arange(DRAFT, dtype=jnp.int32)
    offs = jax.random.randint(base, (REQS, DRAFT), 0, tpos[None, :] + 1).astype(jnp.int32)
    return offs.at[0, DRAFT - 1].set(DRAFT - 1)


def block_levels(stream_key, shape, cuts, low, high):
    def one(position, parts):
        steps = jax.random.uniform(jax.random.fold_in(jax.random.fold_in(stream_key, 6), position), (parts,), jnp.float32, low / len(cuts), high / len(cuts))
        return jnp.repeat(jnp.exp(steps), shape[position] // parts).reshape((-1,) + (1,) * (len(shape) - position - 1))

    level = one(*cuts[0])
    for cut in cuts[1:]:
        level = level * one(*cut)
    return level


def gaussian(key, dims, scale, limit, shards=(), held_as=jnp.bfloat16):
    result = jax.random.normal(key, dims, jnp.float32) * scale
    if len(shards) > 0:
        result = block_levels(key, dims, shards, -0.22, 0.18) * result
    return jnp.clip(result, min=-limit, max=limit).astype(held_as)


def setup_inputs(seed: int = 0) -> dict:
    arg_keys = jax.random.split(jax.random.key(seed), 12)
    return {
        "queries": draw_queries(jax.random.fold_in(arg_keys[11], 71), 0),
        "draft_keys": gaussian(arg_keys[1], (TOKENS, KVH * HD), 0.3, 2.5, ((0, 8), (1, 4))),
        "draft_values": gaussian(arg_keys[2], (TOKENS, KVH * HD), 1.0, 6.0, ((0, 8), (1, 4))),
        "cache_keys": draw_cache_keys(jax.random.fold_in(arg_keys[11], 71), 0),
        "cache_values": gaussian(arg_keys[4], (NBLK, BLK, KVH, HD), 1.0, 6.0, ((0, 8), (2, 4))),
        "w_out": gaussian(arg_keys[5], (QH * HD, D), (QH * HD) ** -0.5, 0.078125, ((0, 4), (1, 8))),
        "lengths": draw_lengths(jax.random.fold_in(arg_keys[11], 71), 0),
        "block_req": draw_block_req(jax.random.fold_in(arg_keys[11], 71), 0),
        "block_idx": draw_block_idx(jax.random.fold_in(arg_keys[11], 71), 0),
        "move_dst": draw_move_dst(jax.random.fold_in(arg_keys[11], 71), 0),
        "draft_offs": draw_draft_offs(jax.random.fold_in(arg_keys[11], 71), 0),
    }


def live_tokens(lengths, block_req, block_idx):
    own_len = jnp.take(lengths, block_req) - block_idx * BLK
    counts = jnp.where(block_idx >= 0, jnp.clip(own_len, 0, BLK), 0)
    return jnp.arange(BLK, dtype=jnp.int32)[None, :] < counts[:, None]

def draft_seen(draft_offs):
    tpos = jnp.arange(DRAFT, dtype=jnp.int32)
    return (tpos[None, None, :] >= draft_offs[:, :, None]) & (tpos[None, None, :] <= tpos[None, :, None])

def relocate(cache, move_dst):
    every = jnp.arange(NBLK, dtype=jnp.int32)
    moved = move_dst >= 0
    earlier = (move_dst[:, None] == move_dst[None, :]) & (every[None, :] < every[:, None])
    order = lax.optimization_barrier(jnp.sum(earlier.astype(jnp.int32), axis=1))
    width = BLOCKS_DEV + IN_DEV
    home = every // BLOCKS_DEV * width + every % BLOCKS_DEV
    away = jnp.where(moved, move_dst * width + BLOCKS_DEV + order, N_CTX * width)
    kept = jnp.where(moved[:, None, None, None], jnp.zeros_like(cache), cache)
    fresh = jnp.zeros((N_CTX * width,) + cache.shape[1:], cache.dtype)
    fresh = fresh.at[home].set(kept)
    return fresh.at[away].set(cache, mode='drop')

def reference(queries, draft_keys, draft_values, cache_keys, cache_values, w_out, lengths, block_req, block_idx, move_dst, draft_offs):
    scale = 1.0 / math.sqrt(HD)
    live = live_tokens(lengths, block_req, block_idx)
    seen = draft_seen(draft_offs)
    onehot = block_req[None, :] == jnp.arange(REQS, dtype=jnp.int32)[:, None]
    onehot_f = onehot.astype(jnp.float32)
    q_heads = jnp.transpose(queries.reshape(REQS, DRAFT, KVH, GROUP, HD), (2, 0, 1, 3, 4))
    k_heads = jnp.transpose(cache_keys, (2, 0, 1, 3))
    v_heads = jnp.transpose(cache_values, (2, 0, 1, 3))
    dk_heads = jnp.transpose(draft_keys.reshape(REQS, DRAFT, KVH, HD), (2, 0, 1, 3))
    dv_heads = jnp.transpose(draft_values.reshape(REQS, DRAFT, KVH, HD), (2, 0, 1, 3))

    def one_head(items):
        q_one, k_one, v_one, dk_one, dv_one = items
        q_slot = jnp.take(q_one, block_req, axis=0)
        scores = jnp.einsum('btgd,bjd->btgj', q_slot.astype(jnp.float32), k_one.astype(jnp.float32)) * scale
        scores = jnp.where(live[:, None, None, :], scores, -jnp.inf)
        block_top = lax.optimization_barrier(jnp.max(scores, axis=3))
        cache_top = lax.optimization_barrier(jnp.max(jnp.where(onehot[:, :, None, None], block_top[None], -jnp.inf), axis=1))
        dscores = jnp.einsum('rtgd,rud->rtgu', q_one.astype(jnp.float32), dk_one.astype(jnp.float32)) * scale
        dscores = jnp.where(seen[:, :, None, :], dscores, -jnp.inf)
        top = jnp.maximum(cache_top, lax.optimization_barrier(jnp.max(dscores, axis=3)))
        probs = jnp.where(live[:, None, None, :], jnp.exp(scores - jnp.take(top, block_req, axis=0)[..., None]), 0.0)
        dprobs = jnp.where(seen[:, :, None, :], jnp.exp(dscores - top[..., None]), 0.0)
        denom = jnp.einsum('rb,btg->rtg', onehot_f, lax.optimization_barrier(jnp.sum(probs, axis=3)), precision=lax.Precision.HIGHEST) + lax.optimization_barrier(jnp.sum(dprobs, axis=3))
        pbf = probs.astype(jnp.bfloat16).astype(jnp.float32)
        slot_numer = jnp.einsum('btgj,bjd->btgd', pbf, v_one.astype(jnp.float32))
        numer = jnp.einsum('rb,btgd->rtgd', onehot_f, slot_numer, precision=lax.Precision.HIGHEST)
        dpbf = dprobs.astype(jnp.bfloat16).astype(jnp.float32)
        numer = numer + jnp.einsum('rtgu,rud->rtgd', dpbf, dv_one.astype(jnp.float32))
        return (numer / denom[..., None]).astype(jnp.bfloat16)
    heads_out = lax.map(one_head, (q_heads, k_heads, v_heads, dk_heads, dv_heads))
    attn = jnp.transpose(heads_out, (1, 2, 0, 3, 4)).reshape(TOKENS, QH * HD)
    mixed = jnp.dot(attn, w_out, preferred_element_type=jnp.float32).astype(jnp.bfloat16)
    return (mixed, relocate(cache_keys, move_dst), relocate(cache_values, move_dst))
```

```python
import functools
import math

import jax
import jax.numpy as jnp
from jax import lax
from jax.experimental import pallas as pl
from jax.experimental.pallas import tpu as pltpu
from jax.sharding import PartitionSpec as P

CAP = 2
SHARE = 6
STEP = 16
TOGETHER = 4
LANES = 16
NEG = -1e30
MESH = pl.DeviceIdType.MESH
VMEM = pl.BlockSpec(memory_space=pltpu.VMEM)
SMEM = pl.BlockSpec(memory_space=pltpu.SMEM)
ANY = pl.BlockSpec(memory_space=pl.ANY)


def greet(axes):
    barrier = pltpu.get_barrier_semaphore()
    total = 0
    for axis, size in axes:
        me = lax.axis_index(axis)
        for d in range(1, size):
            pl.semaphore_signal(
                barrier, inc=1, device_id={axis: lax.rem(me + d, size)}, device_id_type=MESH
            )
        total += size - 1
    pl.semaphore_wait(barrier, total)


def remote(src, dst, send, recv, axis, to):
    return pltpu.make_async_remote_copy(
        src_ref=src, dst_ref=dst, send_sem=send, recv_sem=recv, device_id={axis: to}, device_id_type=MESH
    )


def spread(n, parts, send_sem, recv_sem, pair_send, pair_recv):
    me = lax.axis_index("ctx")
    half = n // 2
    row, side = me // 2, lax.rem(me, 2)
    partner = row * 2 + 1 - side
    started = []
    for a, (src, dst) in enumerate(parts):
        for d in range(1, half):
            to = lax.rem(row + d, half) * 2 + side
            c = remote(src, dst.at[me], send_sem.at[a, d], recv_sem.at[a, d], "ctx", to)
            c.start()
            started.append(c)
        c = remote(src, dst.at[me], pair_send.at[a, 0], pair_recv.at[a, 0], "ctx", partner)
        c.start()
        started.append(c)
    for d in range(1, half):
        for a, (src, dst) in enumerate(parts):
            origin = lax.rem(row + half - d, half) * 2 + side
            remote(src, dst.at[origin], send_sem.at[a, d], recv_sem.at[a, d], "ctx", partner).wait_recv()
            c = remote(
                dst.at[origin], dst.at[origin], pair_send.at[a, d], pair_recv.at[a, d], "ctx", partner
            )
            c.start()
            started.append(c)
    for d in range(half):
        for a, (src, dst) in enumerate(parts):
            origin = lax.rem(row + half - d, half) * 2 + 1 - side
            remote(src, dst.at[origin], pair_send.at[a, d], pair_recv.at[a, d], "ctx", partner).wait_recv()
    for c in started:
        c.wait_send()


def spread_sems(n, count):
    half = n // 2
    return [pltpu.SemaphoreType.DMA((count, half))] * 4


def gather_kernel(n, count, *refs):
    srcs, dsts, sems = refs[:count], refs[count : 2 * count], refs[2 * count :]
    local = sems[4]
    greet([("ctx", n)])
    me = lax.axis_index("ctx")
    own = []
    for a in range(count):
        c = pltpu.make_async_copy(srcs[a], dsts[a].at[me], local.at[a])
        c.start()
        own.append(c)
    spread(n, list(zip(srcs, dsts)), *sems[:4])
    for c in own:
        c.wait()


def gather_all(n, arrays):
    count = len(arrays)
    return pl.pallas_call(
        functools.partial(gather_kernel, n, count),
        out_shape=[jax.ShapeDtypeStruct((n,) + x.shape, x.dtype) for x in arrays],
        in_specs=[VMEM] * count,
        out_specs=[VMEM] * count,
        scratch_shapes=spread_sems(n, count) + [pltpu.SemaphoreType.DMA((count,))],
        compiler_params=pltpu.CompilerParams(collective_id=0, has_side_effects=True),
        name="gather_queries",
    )(*arrays)


def first_share(rows):
    return 2 * rows * SHARE // 8


def pieces(rows, k, v, big, small):
    cut = first_share(rows) - rows
    return (
        (k, big.at[pl.ds(0, rows)]),
        (v.at[pl.ds(0, cut)], big.at[pl.ds(rows, cut)]),
        (v.at[pl.ds(cut, rows - cut)], small),
    )


def pack_kernel(blocks, n, rank_ref, dst_ref, k_ref, v_ref, big_ref, small_ref, seen, sem):
    rows = k_ref.shape[1]
    base = rank_ref[0] * blocks
    for d in range(n):
        seen[d] = 0

    def start(s, count):
        d = dst_ref[base + s]

        @pl.when(d >= 0)
        def _():
            row = d * CAP + seen[d]
            seen[d] = seen[d] + 1
            for src, dst in pieces(rows, k_ref.at[s], v_ref.at[s], big_ref.at[row], small_ref.at[row]):
                pltpu.make_async_copy(src, dst, sem).start()

        return count + (d >= 0).astype(jnp.int32)

    total = lax.fori_loop(0, blocks, start, 0, unroll=8)

    def finish(s, _):
        for src, dst in pieces(rows, k_ref.at[0], v_ref.at[0], big_ref.at[0], small_ref.at[0]):
            pltpu.make_async_copy(src, dst, sem).wait()
        return 0

    lax.fori_loop(0, total, finish, 0)


def pack(n, rank, move_dst, keys, values):
    blocks, rows, lanes = keys.shape
    first = first_share(rows)
    return pl.pallas_call(
        functools.partial(pack_kernel, blocks, n),
        out_shape=[
            jax.ShapeDtypeStruct((n * CAP, first, lanes), keys.dtype),
            jax.ShapeDtypeStruct((n * CAP, 2 * rows - first, lanes), keys.dtype),
        ],
        in_specs=[SMEM, SMEM, ANY, ANY],
        out_specs=[VMEM, VMEM],
        scratch_shapes=[pltpu.SMEM((n,), jnp.int32), pltpu.SemaphoreType.DMA],
        compiler_params=pltpu.CompilerParams(vmem_limit_bytes=60 * 1024 * 1024),
        name="pack_moves",
    )(rank, move_dst, keys, values)


def unpack_kernel(blocks, n, lanes, cnt_ref, big_ref, small_ref, nk_in, nv_in, nk_ref, nv_ref, stage, at, in_sem, out_sem):
    at[0] = 0
    per = lanes // blocks
    rows = stage.shape[2]
    outs = (nk_ref, nv_ref)

    def fetch(row, k):
        parts = pieces(rows, stage.at[0, k], stage.at[1, k], big_ref.at[row], small_ref.at[row])
        return [pltpu.make_async_copy(src, dst, in_sem.at[k, x]) for x, (dst, src) in enumerate(parts)]

    def place(a, k):
        return pltpu.make_async_copy(stage.at[a, k], outs[a].at[blocks + k], out_sem)

    for src in range(n):
        for j in range(CAP):

            @pl.when((j < cnt_ref[src // per, src % per]) & (at[0] < n))
            def _():
                for c in fetch(src * CAP + j, at[0]):
                    c.start()
                at[0] = at[0] + 1

    total = at[0]

    def store(k, _):
        for c in fetch(0, k):
            c.wait()
        for a in range(2):
            place(a, k).start()
        return 0

    lax.fori_loop(0, total, store, 0)

    def finish(k, _):
        for a in range(2):
            place(a, 0).wait()
        return 0

    lax.fori_loop(0, total, finish, 0)


def unpack(n, blocks, arriving, big, small, new_keys, new_values):
    rows, lanes = new_keys.shape[1:]
    return pl.pallas_call(
        functools.partial(unpack_kernel, blocks, n, lanes),
        out_shape=[jax.ShapeDtypeStruct(x.shape, x.dtype) for x in (new_keys, new_values)],
        in_specs=[SMEM, ANY, ANY, ANY, ANY],
        out_specs=[ANY, ANY],
        input_output_aliases={3: 0, 4: 1},
        scratch_shapes=[
            pltpu.VMEM((2, n, rows, lanes), new_keys.dtype),
            pltpu.SMEM((1,), jnp.int32),
            pltpu.SemaphoreType.DMA((n, 3)),
            pltpu.SemaphoreType.DMA,
        ],
        compiler_params=pltpu.CompilerParams(vmem_limit_bytes=60 * 1024 * 1024),
        name="place_moves",
    )(arriving, big, small, new_keys, new_values)


def attend_kernel(
    dims,
    rank_ref,
    req_ref,
    idx_ref,
    dst_ref,
    len_ref,
    q_hbm,
    k_hbm,
    v_hbm,
    dk_ref,
    dv_ref,
    offs_ref,
    plan_ref,
    nk_ref,
    nv_ref,
    o_ref,
    lse_ref,
    arr_ref,
    q_ref,
    k_ref,
    v_ref,
    tok_ref,
    acc,
    den,
    top,
    zero,
    q_sem,
    in_sem,
    out_sem,
    zero_sem,
):
    n, blocks, width, kv, heads, hd, drafts, requests, own, aligned, steps, per_chunk = dims
    group = heads // kv
    part_rows = group * drafts
    rows = width * kv
    rank = rank_ref[0]
    base = rank * blocks
    outs = ((k_hbm, k_ref, nk_ref), (v_hbm, v_ref, nv_ref))

    def load(a, i):
        span = pl.ds(i * STEP, STEP)
        return pltpu.make_async_copy(outs[a][0].at[span], outs[a][1].at[span], in_sem.at[a, i])

    ask = pltpu.make_async_copy(q_hbm, q_ref, q_sem)
    ask.start()
    for i in range(steps):
        for a in range(2):
            load(a, i).start()
    factor = math.log2(math.e) / math.sqrt(hd)
    nt = (((1,), (1,)), ((), ()))

    def query(r):
        q = q_ref[pl.ds(pl.multiple_of(r * drafts, drafts), drafts), :]
        return jnp.concatenate([q[:, h * hd : (h + 1) * hd] for h in range(heads)], axis=0)

    def weighed(r, lo, size, counts):
        k = k_ref[pl.ds(lo, size)].reshape(size * rows, hd)
        v = v_ref[pl.ds(lo, size)].reshape(size * rows, hd)
        s = lax.dot_general(query(r), k, nt, preferred_element_type=jnp.float32) * factor
        tok = tok_ref[...]
        s = [jnp.where(tok < c, s[:, x * rows : (x + 1) * rows], NEG) for x, c in enumerate(counts)]
        m = jnp.max(functools.reduce(jnp.maximum, s), axis=1, keepdims=True)
        p = [jnp.exp2(x - m) for x in s]
        mass = jnp.sum(functools.reduce(jnp.add, p), axis=1, keepdims=True)
        p = jnp.concatenate([x.astype(jnp.bfloat16) for x in p], axis=1)
        return m, mass, jnp.dot(p, v, preferred_element_type=jnp.float32)

    def merge(r, m, mass, o):
        old = top[r]
        new = jnp.maximum(old, m)
        a, b = jnp.exp2(old - new), jnp.exp2(m - new)
        top[r] = new
        den[r] = den[r] * a + mass * b
        acc[r] = acc[r] * a + o * b

    def settled(i):
        stay = dst_ref[base + i * STEP] < 0
        for b in range(1, STEP):
            stay = stay & (dst_ref[base + i * STEP + b] < 0)
        return stay

    def all_out(a, i):
        span = pl.ds(i * STEP, STEP)
        return pltpu.make_async_copy(outs[a][1].at[span], outs[a][2].at[span], out_sem.at[a, i * STEP])

    def one_out(a, s, blank):
        return pltpu.make_async_copy(zero.at[0] if blank else outs[a][1].at[s], outs[a][2].at[s], out_sem.at[a, s])

    def blank_tail(a, x):
        return pltpu.make_async_copy(zero.at[pl.ds(0, 8)], outs[a][2].at[pl.ds(blocks + x * 8, 8)], zero_sem.at[a, x])

    zero[...] = jnp.zeros_like(zero)
    for a in range(2):
        for x in range(n // 8):
            blank_tail(a, x).start()
    side = lax.broadcasted_iota(jnp.int32, tok_ref.shape, 0) // part_rows
    col = lax.broadcasted_iota(jnp.int32, tok_ref.shape, 1)
    tok_ref[...] = jnp.where(side == col % kv, col // kv, width)
    top[...] = jnp.full_like(top, NEG)
    acc[...] = jnp.zeros_like(acc)
    den[...] = jnp.zeros_like(den)
    mine = (plan_ref[...] == rank).astype(jnp.int32)
    lane = lax.broadcasted_iota(jnp.int32, plan_ref.shape, 1)
    come = jnp.zeros_like(mine)
    for x in range(hd // blocks):
        some = jnp.sum(jnp.where(lane // blocks == x, mine, 0), axis=1, keepdims=True)
        come = jnp.where(lane == x, some, come)
    arr_ref[...] = come
    ask.wait()
    line = lax.broadcasted_iota(jnp.int32, (drafts, requests), 1)
    t = lax.broadcasted_iota(jnp.int32, (drafts, kv * drafts), 0)
    u = lax.broadcasted_iota(jnp.int32, (drafts, kv * drafts), 1)

    def draft(x):
        r = rank * own + x if aligned else rank + n * x
        place = x * drafts if aligned else pl.multiple_of(r * drafts, drafts)
        dk = dk_ref[pl.ds(place, drafts), :]
        dv = dv_ref[pl.ds(place, drafts), :]
        dk = jnp.concatenate([dk[:, g * hd : (g + 1) * hd] for g in range(kv)], axis=0)
        dv = jnp.concatenate([dv[:, g * hd : (g + 1) * hd] for g in range(kv)], axis=0)
        s = lax.dot_general(query(r), dk, nt, preferred_element_type=jnp.float32) * factor
        off = jnp.sum(jnp.where(line == r, offs_ref[...], 0), axis=1, keepdims=True)
        seen = (u % drafts >= off) & (u % drafts <= t)
        bias = jnp.concatenate(
            [jnp.where(seen & (u // drafts == h // group), 0.0, NEG) for h in range(heads)], axis=0
        )
        s = jnp.where(bias < 0, NEG, s)
        m = jnp.max(s, axis=1, keepdims=True)
        p = jnp.exp2(s - m)
        top[r] = jnp.broadcast_to(m, top.shape[1:])
        den[r] = jnp.broadcast_to(jnp.sum(p, axis=1, keepdims=True), den.shape[1:])
        acc[r] = jnp.dot(p.astype(jnp.bfloat16), dv, preferred_element_type=jnp.float32)

    for x in range(own):
        if aligned:
            draft(x)
        else:
            pl.when(rank + n * x < requests)(functools.partial(draft, x))

    def step(i, _):
        calm = settled(i)
        for a in range(2):
            load(a, i).wait()

        @pl.when(calm)
        def _():
            for a in range(2):
                all_out(a, i).start()

        @pl.when(jnp.logical_not(calm))
        def _():
            for b in range(STEP):
                s = i * STEP + b
                kept = dst_ref[base + s] < 0
                for blank in (False, True):

                    @pl.when(kept != blank)
                    def _():
                        for a in range(2):
                            one_out(a, s, blank).start()

        first = i * STEP
        reqs = [req_ref[base + first + b] for b in range(STEP)]
        counts = []
        for b, r in enumerate(reqs):
            x = idx_ref[base + first + b]
            counts.append(jnp.where(x >= 0, jnp.clip(len_ref[r] - x * width, 0, width), 0))

        def alike(lo, size):
            same = jnp.bool_(True)
            for b in range(lo + 1, lo + size):
                same = same & ((reqs[b] == reqs[lo]) | (counts[b] == 0))
            return same

        def joint(lo, size):
            merge(reqs[lo], *weighed(reqs[lo], first + lo, size, counts[lo : lo + size]))

        def single(lo, size):
            some = range(lo, lo + size)
            found = [weighed(reqs[b], first + b, 1, [counts[b]]) for b in some]
            for b, parts in zip(some, found):
                merge(reqs[b], *parts)

        @pl.when(counts[0] > 0)
        def _():
            for lo in range(0, STEP, TOGETHER):
                single(lo, TOGETHER)

        return 0

    lax.fori_loop(0, steps, step, 0)
    lane = lax.broadcasted_iota(jnp.int32, (drafts, hd), 1)
    if o_ref.shape[0] > requests * drafts:
        rest = pl.ds(requests * drafts, o_ref.shape[0] - requests * drafts)
        o_ref[rest, :] = jnp.zeros_like(o_ref[rest, :])
    lse_ref[...] = jnp.full_like(lse_ref, NEG)

    def close(r, _):
        place = pl.ds(pl.multiple_of(r * drafts, drafts), drafts)
        spot = lax.rem(r, per_chunk) * LANES
        high = jnp.full((drafts, hd), NEG, jnp.float32)
        mass = jnp.ones((drafts, hd), jnp.float32)
        for h in range(heads):
            at = slice(h * drafts, (h + 1) * drafts)
            total = den[r, at, :]
            dead = total <= 0
            o = acc[r, at, :] * jnp.where(dead, 0.0, 1.0 / jnp.where(dead, 1.0, total))
            o_ref[place, h * hd : (h + 1) * hd] = o.astype(jnp.bfloat16)
            high = jnp.where(lane == spot + h, top[r, at, :], high)
            mass = jnp.where(lane == spot + h, total, mass)
        dead = mass <= 0
        level = jnp.where(dead, NEG, high + jnp.log2(jnp.where(dead, 1.0, mass)))
        line = pl.ds(pl.multiple_of(r // per_chunk * drafts, drafts), drafts)
        lse_ref[line, :] = jnp.where((lane >= spot) & (lane < spot + heads), level, lse_ref[line, :])
        return 0

    lax.fori_loop(0, requests, close, 0, unroll=4)

    def finish(i, _):
        calm = settled(i)

        @pl.when(calm)
        def _():
            for a in range(2):
                all_out(a, i).wait()

        @pl.when(jnp.logical_not(calm))
        def _():
            for b in range(STEP):
                for a in range(2):
                    one_out(a, i * STEP + b, False).wait()

        return 0

    lax.fori_loop(0, steps, finish, 0)
    for a in range(2):
        for x in range(n // 8):
            blank_tail(a, x).wait()


def attend(n, rank, tables, q_all, keys, values, dk, dv, offs, plan, kv, out_rows, aligned, own):
    blocks, rows, hd = keys.shape
    width = rows // kv
    block_req, block_idx, move_dst, lengths = tables
    drafts, requests = offs.shape
    heads = q_all.shape[1] // hd
    steps = blocks // STEP
    qrows = heads * drafts
    per_chunk = out_rows // n // drafts
    dims = (n, blocks, width, kv, heads, hd, drafts, requests, own, aligned, steps, per_chunk)
    grown = jax.ShapeDtypeStruct((blocks + n, rows, hd), keys.dtype)
    o = jax.ShapeDtypeStruct((out_rows, heads * hd), jnp.bfloat16)
    lse = jax.ShapeDtypeStruct((n * drafts, hd), jnp.float32)
    arr = jax.ShapeDtypeStruct(plan.shape, jnp.int32)
    dma = pltpu.SemaphoreType.DMA
    return pl.pallas_call(
        functools.partial(attend_kernel, dims),
        out_shape=[grown, grown, o, lse, arr],
        in_specs=[SMEM] * 5 + [ANY] * 3 + [VMEM] * 4,
        out_specs=[ANY, ANY, VMEM, VMEM, VMEM],
        scratch_shapes=[
            pltpu.VMEM(q_all.shape, q_all.dtype),
            pltpu.VMEM(keys.shape, keys.dtype),
            pltpu.VMEM(keys.shape, keys.dtype),
            pltpu.VMEM((qrows, rows), jnp.int32),
            pltpu.VMEM((requests, qrows, hd), jnp.float32),
            pltpu.VMEM((requests, qrows, hd), jnp.float32),
            pltpu.VMEM((requests, qrows, hd), jnp.float32),
            pltpu.VMEM((STEP, rows, hd), keys.dtype),
            dma,
            dma((2, steps)),
            dma((2, blocks)),
            dma((2, n // 8)),
        ],
        compiler_params=pltpu.CompilerParams(vmem_limit_bytes=60 * 1024 * 1024),
        cost_estimate=pl.CostEstimate(
            flops=4 * blocks * qrows * rows * hd, bytes_accessed=8 * blocks * rows * hd, transcendentals=0
        ),
        name="attend",
    )(rank, block_req, block_idx, move_dst, lengths, q_all, keys, values, dk, dv, offs, plan)


def merge_parts(parts, out, level_out, heads, hd):
    levels = [level for _, level in parts]
    drafts = levels[0].shape[0]
    best = functools.reduce(jnp.maximum, levels)
    weights = [jnp.exp2(x - best) for x in levels]
    mass = functools.reduce(jnp.add, weights)
    norm = 1.0 / mass
    weights = [x * norm for x in weights]
    for x in range(out.shape[0] // drafts):
        place = slice(x * drafts, (x + 1) * drafts)
        for h in range(heads):
            cols = slice(h * hd, (h + 1) * hd)
            lane = x * LANES + h
            total = None
            for (view, _), weight in zip(parts, weights):
                term = weight[:, lane : lane + 1] * view[place, cols].astype(jnp.float32)
                total = term if total is None else total + term
            out[place, cols] = total.astype(jnp.bfloat16)
    if level_out is not None:
        level_out[...] = best + jnp.log2(mass)


def combine_kernel(
    dims,
    o_ref,
    lse_ref,
    w_ref,
    far_ref,
    out_ref,
    come_ref,
    near_o,
    near_l,
    sum_o,
    sum_l,
    line_o,
    line_l,
    attn_own,
    attn,
    part,
    got,
    mix,
    *sems,
):
    n, nh, chunk, heads, hd, rows = dims
    nos, nor, nls, nlr, los, lor, lls, llr, ups, dns, zr, ps, pr, hs, hr, ms, mr, local = sems
    half = n // 2
    me = lax.axis_index("ctx")
    hme = lax.axis_index("head")
    row, side = me // 2, lax.rem(me, 2)
    partner = row * 2 + 1 - side
    greet([("ctx", n), ("head", nh)])
    low = row < half // 2
    own_turn = jnp.where(low, half - 1 - row, row)

    def turn(k):
        x = k + jnp.where(k >= own_turn, 1, 0)
        return jnp.where(low, half - 1 - x, x)

    def near(r):
        c = r * 2 + 1 - side
        return (
            remote(lse_ref.at[c], near_l.at[r], nls.at[r], nlr.at[r], "ctx", partner),
            remote(o_ref.at[c], near_o.at[r], nos.at[r], nor.at[r], "ctx", partner),
        )

    def along(r):
        to = jnp.where(r > row, row + 1, row - 1)
        slot = jnp.where((r < row) & (to == r), half, r)
        return (
            remote(sum_l.at[r], line_l.at[slot], lls.at[r], llr.at[slot], "ctx", to * 2 + side),
            remote(sum_o.at[r], line_o.at[slot], los.at[r], lor.at[slot], "ctx", to * 2 + side),
        )

    def arrived(slot):
        remote(sum_l.at[0], line_l.at[slot], lls.at[0], llr.at[slot], "ctx", partner).wait_recv()
        remote(sum_o.at[0], line_o.at[slot], los.at[0], lor.at[slot], "ctx", partner).wait_recv()

    def relocate(d):
        dst = come_ref.at[pl.ds(me * CAP, CAP)]
        return remote(far_ref.at[pl.ds(d * CAP, CAP)], dst, ms.at[d], mr.at[me], "ctx", d)

    def relocated(d):
        dst = come_ref.at[pl.ds(d * CAP, CAP)]
        return remote(far_ref.at[pl.ds(d * CAP, CAP)], dst, ms.at[d], mr.at[d], "ctx", partner)

    def blank(slot):
        line_l[slot] = jnp.full(line_l.shape[1:], NEG, jnp.float32)
        line_o[slot] = jnp.zeros(line_o.shape[1:], line_o.dtype)

    for k in range(half - 1):
        for c in near(turn(k)):
            c.start()
    for c in near(row):
        c.start()

    @pl.when(row == 0)
    def _():
        for r in range(half):
            blank(r)

    @pl.when(row == half - 1)
    def _():
        for r in range(half - 1):
            blank(r)
        blank(half)

    def reduce(k, _):
        r = turn(k)
        for c in near(r):
            c.wait_recv()

        @pl.when(jnp.where(r > row, row > 0, row < half - 1))
        def _():
            arrived(r)

        at = r * 2 + side
        merge_parts(
            [(o_ref.at[at], lse_ref[at]), (near_o.at[r], near_l[r]), (line_o.at[r], line_l[r])],
            sum_o.at[r],
            sum_l.at[r],
            heads,
            hd,
        )
        for c in along(r):
            c.start()
        return 0

    lax.fori_loop(0, half - 1, reduce, 0)
    relocate(partner).start()
    for c in near(row):
        c.wait_recv()

    @pl.when(row > 0)
    def _():
        arrived(row)

    @pl.when(row < half - 1)
    def _():
        arrived(half)

    merge_parts(
        [
            (o_ref.at[me], lse_ref[me]),
            (near_o.at[row], near_l[row]),
            (line_o.at[row], line_l[row]),
            (line_o.at[half], line_l[half]),
        ],
        attn_own,
        None,
        heads,
        hd,
    )
    mine = pltpu.make_async_copy(attn_own, attn.at[me], local)
    mine.start()

    def upward(r):
        src = attn.at[r * 2 + side]
        return remote(src, src, ups.at[r], zr.at[r], "ctx", (row + 1) * 2 + side)

    def downward(r):
        src = attn.at[r * 2 + side]
        return remote(src, src, dns.at[r], zr.at[r], "ctx", (row - 1) * 2 + side)

    def across(r):
        src = attn.at[r * 2 + side]
        return remote(src, src, ps.at[r], pr.at[r], "ctx", partner)

    def crossed(r):
        dst = attn.at[r * 2 + 1 - side]
        remote(attn_own, dst, ps.at[r], pr.at[r], "ctx", partner).wait_recv()

    w = w_ref[...]

    def project(j):
        e = lax.rem(j + nh - hme, nh)
        value = jnp.dot(
            attn_rows(attn, pl.multiple_of(j * rows, 16), rows, chunk), w, preferred_element_type=jnp.float32
        )

        @pl.when(e == 0)
        def _():
            mix[...] = value

        @pl.when(e != 0)
        def _():
            part[e] = value.astype(jnp.bfloat16)
            remote(part.at[e], got.at[e], hs.at[e], hr.at[e], "head", j).start()

    mine.wait()
    pl.when(row < half - 1)(lambda: upward(row).start())
    pl.when(row > 0)(lambda: downward(row).start())
    across(row).start()
    matched = rows == 2 * chunk and nh == half

    def take(d):
        for r, ok, more, on in (
            (row - d, row >= d, row < half - 1, upward),
            (row + d, row + d < half, row > 0, downward),
        ):

            @pl.when(ok)
            def _():
                remote(attn_own, attn.at[r * 2 + side], ups.at[r], zr.at[r], "ctx", partner).wait_recv()
                pl.when(more)(lambda: on(r).start())
                across(r).start()

    def use(d):
        for r, ok in ((row - d, row >= d), (row + d, row + d < half)):

            @pl.when(ok)
            def _():
                crossed(r)
                project(r)

    for d in range(1, half):
        take(d)
        if d == half - 1:
            for x in range(n):
                pl.when(row != x // 2)(lambda: relocate(x).start())
        if matched:
            if d == 1:
                crossed(row)
                project(row)
            else:
                use(d - 1)
    if matched:
        use(half - 1)
    else:
        for r in range(half):
            crossed(r)
        for d in range(nh):
            project(lax.rem(hme + 1 + d, nh))
    total = mix[...]
    for e in range(1, nh):
        c = remote(part.at[e], got.at[e], hs.at[e], hr.at[e], "head", lax.rem(hme + e, nh))
        c.wait_recv()
        total += got[e].astype(jnp.float32)
    out_ref[...] = total.astype(jnp.bfloat16)
    for e in range(1, nh):
        remote(part.at[e], got.at[e], hs.at[e], hr.at[e], "head", lax.rem(hme + e, nh)).wait_send()
    for k in range(half - 1):
        r = turn(k)
        for c in near(r) + along(r):
            c.wait_send()
    for c in near(row):
        c.wait_send()
    for r in range(half):
        pl.when((row < half - 1) & (r <= row))(lambda: upward(r).wait_send())
        pl.when((row > 0) & (r >= row))(lambda: downward(r).wait_send())
        across(r).wait_send()
    for x in range(n):

        @pl.when(me != x)
        def _():
            relocate(x).wait_send()
            relocated(x).wait_recv()


def attn_rows(attn, start, rows, chunk):
    piece = math.gcd(rows, chunk)
    out = []
    for x in range(rows // piece):
        at = start + x * piece
        out.append(attn[at // chunk, pl.ds(pl.multiple_of(lax.rem(at, chunk), 16), piece), :])
    return jnp.concatenate(out, axis=0)


def combine(n, nh, o, lse, w, far, tokens):
    _, chunk, cols = o.shape
    drafts, hd = lse.shape[1:]
    heads = cols // hd
    rows = tokens // nh
    wide = w.shape[1]
    half = n // 2
    dims = (n, nh, chunk, heads, hd, rows)
    dma = pltpu.SemaphoreType.DMA
    outs = lambda count: pltpu.VMEM((count, chunk, cols), jnp.bfloat16)
    levels = lambda count: pltpu.VMEM((count, drafts, hd), jnp.float32)
    return pl.pallas_call(
        functools.partial(combine_kernel, dims),
        out_shape=[jax.ShapeDtypeStruct((rows, wide), jnp.bfloat16), jax.ShapeDtypeStruct(far.shape, far.dtype)],
        in_specs=[VMEM] * 3 + [ANY],
        out_specs=[VMEM, ANY],
        scratch_shapes=[outs(half), levels(half), outs(half), levels(half), outs(half + 1), levels(half + 1)]
        + [
            pltpu.VMEM((chunk, cols), jnp.bfloat16),
            pltpu.VMEM((n, chunk, cols), jnp.bfloat16),
            pltpu.VMEM((nh, rows, wide), jnp.bfloat16),
            pltpu.VMEM((nh, rows, wide), jnp.bfloat16),
            pltpu.VMEM((rows, wide), jnp.float32),
        ]
        + [dma((half,))] * 4
        + [dma((half + 1,))] * 4
        + [dma((half,))] * 5
        + [dma((nh,))] * 2
        + [dma((n,))] * 2
        + [dma],
        compiler_params=pltpu.CompilerParams(
            collective_id=1, has_side_effects=True, vmem_limit_bytes=60 * 1024 * 1024
        ),
        name="combine",
    )(o, lse, w, far)


def shards(
    n,
    nh,
    queries,
    draft_keys,
    draft_values,
    cache_keys,
    cache_values,
    w_out,
    lengths,
    block_req,
    block_idx,
    move_dst,
    draft_offs,
):
    blocks, width, kv, hd = cache_keys.shape
    requests, drafts = draft_offs.shape
    tokens = requests * drafts
    local_tokens = queries.shape[0]
    heads = queries.shape[1] // hd
    me = lax.axis_index("ctx")
    rank = jnp.reshape(me, (1,)).astype(jnp.int32)
    keys = cache_keys.reshape(blocks, width * kv, hd)
    values = cache_values.reshape(blocks, width * kv, hd)
    big, small = pack(n, rank, move_dst, keys, values)
    big, queries = lax.optimization_barrier((big, queries))

    aligned = local_tokens % drafts == 0
    if aligned:
        own = local_tokens // drafts
        (q_all,) = gather_all(n, [queries])
        dk, dv = draft_keys, draft_values
    else:
        own = -(-requests // n)
        q_all, dk, dv = gather_all(n, [queries, draft_keys, draft_values])
        dk, dv = dk.reshape(tokens, -1), dv.reshape(tokens, -1)
    big, q_all = lax.optimization_barrier((big, q_all))
    big = lax.all_to_all(big, "ctx", split_axis=0, concat_axis=0, tiled=True)
    q_all = q_all.reshape(tokens, heads * hd)
    chunk = -(-requests // n) * drafts
    new_keys, new_values, o, lse, arriving = attend(
        n,
        rank,
        (block_req, block_idx, move_dst, lengths),
        q_all,
        keys,
        values,
        dk,
        dv,
        draft_offs.T,
        move_dst.reshape(-1, hd),
        kv,
        n * chunk,
        aligned,
        own,
    )
    mixed, small = combine(n, nh, o.reshape(n, chunk, -1), lse.reshape(n, drafts, hd), w_out, small, tokens)
    new_keys, new_values = unpack(n, blocks, arriving, big, small, new_keys, new_values)
    shape = (blocks + n, width, kv, hd)
    return (mixed, new_keys.reshape(shape), new_values.reshape(shape))


def solution(mesh):
    in_specs = (
        P("ctx", "head"),
        P("ctx", "head"),
        P("ctx", "head"),
        P("ctx", None, "head", None),
        P("ctx", None, "head", None),
        P("head", "ctx"),
        P(),
        P(),
        P(),
        P(),
        P(),
    )
    out_specs = (P("head", "ctx"), P("ctx", None, "head", None), P("ctx", None, "head", None))
    body = functools.partial(shards, mesh.shape["ctx"], mesh.shape["head"])
    return jax.shard_map(body, mesh=mesh, in_specs=in_specs, out_specs=out_specs, check_vma=False)
```

```python
import functools
import math

import jax
import jax.numpy as jnp
from jax import lax
from jax.experimental import pallas as pl
from jax.experimental.pallas import tpu as pltpu
from jax.sharding import PartitionSpec as P

CAP = 2
EARLY = 1
SHARE = 5
STEP = 16
TOGETHER = 4
LANES = 16
NEG = -1e30
MESH = pl.DeviceIdType.MESH
VMEM = pl.BlockSpec(memory_space=pltpu.VMEM)
SMEM = pl.BlockSpec(memory_space=pltpu.SMEM)
ANY = pl.BlockSpec(memory_space=pl.ANY)


def greet(axes):
    barrier = pltpu.get_barrier_semaphore()
    total = 0
    for axis, size in axes:
        me = lax.axis_index(axis)
        for d in range(1, size):
            pl.semaphore_signal(
                barrier, inc=1, device_id={axis: lax.rem(me + d, size)}, device_id_type=MESH
            )
        total += size - 1
    pl.semaphore_wait(barrier, total)


def remote(src, dst, send, recv, axis, to):
    return pltpu.make_async_remote_copy(
        src_ref=src, dst_ref=dst, send_sem=send, recv_sem=recv, device_id={axis: to}, device_id_type=MESH
    )


def gather_kernel(n, count, *refs):
    srcs, move_ref = refs[:count], refs[count]
    dsts, come_ref = refs[count + 1 : 2 * count + 1], refs[2 * count + 1]
    ups, dns, zr, ps, pr, ms, mr, local = refs[2 * count + 2 :]
    half = n // 2
    greet([("ctx", n)])
    me = lax.axis_index("ctx")
    row, side = me // 2, lax.rem(me, 2)
    partner = row * 2 + 1 - side

    def send(a, r, sem, to, own):
        at = r * 2 + side
        recv = pr if sem is ps else zr
        return remote(srcs[a] if own else dsts[a].at[at], dsts[a].at[at], sem.at[a, r], recv.at[a, r], "ctx", to)

    def upward(a, r, own=False):
        return send(a, r, ups, (row + 1) * 2 + side, own)

    def downward(a, r, own=False):
        return send(a, r, dns, (row - 1) * 2 + side, own)

    def across(a, r, own=False):
        return send(a, r, ps, partner, own)

    each = range(count)
    for a in each:
        pl.when(row < half - 1)(lambda: upward(a, row, True).start())
        pl.when(row > 0)(lambda: downward(a, row, True).start())
        across(a, row, True).start()
    own = [pltpu.make_async_copy(srcs[a], dsts[a].at[me], local.at[a]) for a in each]
    for c in own:
        c.start()

    def take(d):
        for r, ok, more, on in (
            (row - d, row >= d, row < half - 1, upward),
            (row + d, row + d < half, row > 0, downward),
        ):

            @pl.when(ok)
            def _():
                for a in each:
                    dst = dsts[a].at[r * 2 + side]
                    remote(srcs[a], dst, ups.at[a, r], zr.at[a, r], "ctx", partner).wait_recv()
                    pl.when(more)(lambda: on(a, r).start())
                    across(a, r).start()

    for d in range(1, half):
        take(d)
        if d == max(half - 2, 1):
            for x in range(n):
                pl.when(me != x)(lambda: relocate(move_ref, come_ref, ms, mr, me, x).start())
    for c in own:
        c.wait()
    for r in range(half):
        for a in each:
            dst = dsts[a].at[r * 2 + 1 - side]
            remote(srcs[a], dst, ps.at[a, r], pr.at[a, r], "ctx", partner).wait_recv()
            pl.when((row < half - 1) & (r <= row))(lambda: upward(a, r).wait_send())
            pl.when((row > 0) & (r >= row))(lambda: downward(a, r).wait_send())
            across(a, r).wait_send()
    settle(n, move_ref, come_ref, ms, mr, me, partner)


def relocate(src, dst, send, recv, me, to):
    return remote(src.at[pl.ds(to * CAP, CAP)], dst.at[pl.ds(me * CAP, CAP)], send.at[to], recv.at[me], "ctx", to)


def settle(n, src, dst, send, recv, me, partner):
    for x in range(n):

        @pl.when(me != x)
        def _():
            span = pl.ds(x * CAP, CAP)
            c = remote(src.at[span], dst.at[span], send.at[x], recv.at[x], "ctx", partner)
            c.wait_send()
            c.wait_recv()


def gather_all(n, arrays, moves):
    count = len(arrays)
    dma = pltpu.SemaphoreType.DMA
    return pl.pallas_call(
        functools.partial(gather_kernel, n, count),
        out_shape=[jax.ShapeDtypeStruct((n,) + x.shape, x.dtype) for x in arrays]
        + [jax.ShapeDtypeStruct(moves.shape, moves.dtype)],
        in_specs=[VMEM] * count + [ANY],
        out_specs=[VMEM] * count + [ANY],
        scratch_shapes=[dma((count, n // 2))] * 5 + [dma((n,))] * 2 + [dma((count,))],
        compiler_params=pltpu.CompilerParams(
            collective_id=0, has_side_effects=True, vmem_limit_bytes=60 * 1024 * 1024
        ),
        name="gather_queries",
    )(*arrays, moves)


def shares(rows):
    unit = 2 * rows // 8
    return unit * EARLY, unit * SHARE, unit * (8 - EARLY - SHARE)


def pieces(rows, k, v, early, big, small):
    first, middle, last = shares(rows)
    cut = rows - last
    return (
        (k.at[pl.ds(0, first)], early),
        (k.at[pl.ds(first, rows - first)], big.at[pl.ds(0, rows - first)]),
        (v.at[pl.ds(0, cut)], big.at[pl.ds(rows - first, cut)]),
        (v.at[pl.ds(cut, last)], small),
    )


def pack_kernel(blocks, n, rank_ref, dst_ref, k_ref, v_ref, early_ref, big_ref, small_ref, seen, sem):
    rows = k_ref.shape[1]
    base = rank_ref[0] * blocks
    for d in range(n):
        seen[d] = 0

    def start(s, count):
        d = dst_ref[base + s]

        @pl.when(d >= 0)
        def _():
            row = d * CAP + seen[d]
            seen[d] = seen[d] + 1
            for src, dst in pieces(
                rows, k_ref.at[s], v_ref.at[s], early_ref.at[row], big_ref.at[row], small_ref.at[row]
            ):
                pltpu.make_async_copy(src, dst, sem).start()

        return count + (d >= 0).astype(jnp.int32)

    total = lax.fori_loop(0, blocks, start, 0, unroll=8)

    def finish(s, _):
        for src, dst in pieces(
            rows, k_ref.at[0], v_ref.at[0], early_ref.at[0], big_ref.at[0], small_ref.at[0]
        ):
            pltpu.make_async_copy(src, dst, sem).wait()
        return 0

    lax.fori_loop(0, total, finish, 0)


def pack(n, rank, move_dst, keys, values):
    blocks, rows, lanes = keys.shape
    return pl.pallas_call(
        functools.partial(pack_kernel, blocks, n),
        out_shape=[jax.ShapeDtypeStruct((n * CAP, x, lanes), keys.dtype) for x in shares(rows)],
        in_specs=[SMEM, SMEM, ANY, ANY],
        out_specs=[VMEM] * 3,
        scratch_shapes=[pltpu.SMEM((n,), jnp.int32), pltpu.SemaphoreType.DMA],
        compiler_params=pltpu.CompilerParams(vmem_limit_bytes=60 * 1024 * 1024),
        name="pack_moves",
    )(rank, move_dst, keys, values)


def unpack_kernel(blocks, n, lanes, cnt_ref, early_ref, big_ref, small_ref, nk_in, nv_in, nk_ref, nv_ref, stage, at, in_sem, out_sem):
    at[0] = 0
    per = lanes // blocks
    rows = stage.shape[2]
    outs = (nk_ref, nv_ref)

    def fetch(row, k):
        came = (early_ref.at[row], big_ref.at[row], small_ref.at[row])
        parts = pieces(rows, stage.at[0, k], stage.at[1, k], *came)
        return [pltpu.make_async_copy(src, dst, in_sem.at[k, x]) for x, (dst, src) in enumerate(parts)]

    def place(a, k):
        return pltpu.make_async_copy(stage.at[a, k], outs[a].at[blocks + k], out_sem)

    for src in range(n):
        for j in range(CAP):

            @pl.when((j < cnt_ref[src // per, src % per]) & (at[0] < n))
            def _():
                for c in fetch(src * CAP + j, at[0]):
                    c.start()
                at[0] = at[0] + 1

    total = at[0]

    def store(k, _):
        for c in fetch(0, k):
            c.wait()
        for a in range(2):
            place(a, k).start()
        return 0

    lax.fori_loop(0, total, store, 0)

    def finish(k, _):
        for a in range(2):
            place(a, 0).wait()
        return 0

    lax.fori_loop(0, total, finish, 0)


def unpack(n, blocks, arriving, came, new_keys, new_values):
    rows, lanes = new_keys.shape[1:]
    return pl.pallas_call(
        functools.partial(unpack_kernel, blocks, n, lanes),
        out_shape=[jax.ShapeDtypeStruct(x.shape, x.dtype) for x in (new_keys, new_values)],
        in_specs=[SMEM] + [ANY] * 5,
        out_specs=[ANY, ANY],
        input_output_aliases={4: 0, 5: 1},
        scratch_shapes=[
            pltpu.VMEM((2, n, rows, lanes), new_keys.dtype),
            pltpu.SMEM((1,), jnp.int32),
            pltpu.SemaphoreType.DMA((n, 4)),
            pltpu.SemaphoreType.DMA,
        ],
        compiler_params=pltpu.CompilerParams(vmem_limit_bytes=60 * 1024 * 1024),
        name="place_moves",
    )(arriving, *came, new_keys, new_values)


def attend_kernel(
    dims,
    rank_ref,
    req_ref,
    idx_ref,
    dst_ref,
    len_ref,
    q_hbm,
    k_hbm,
    v_hbm,
    dk_ref,
    dv_ref,
    offs_ref,
    plan_ref,
    nk_ref,
    nv_ref,
    o_ref,
    lse_ref,
    arr_ref,
    q_ref,
    k_ref,
    v_ref,
    tok_ref,
    acc,
    den,
    top,
    zero,
    q_sem,
    in_sem,
    out_sem,
    zero_sem,
):
    n, blocks, width, kv, heads, hd, drafts, requests, own, aligned, steps, per_chunk = dims
    group = heads // kv
    part_rows = group * drafts
    rows = width * kv
    rank = rank_ref[0]
    base = rank * blocks
    outs = ((k_hbm, k_ref, nk_ref), (v_hbm, v_ref, nv_ref))

    def load(a, i):
        span = pl.ds(i * STEP, STEP)
        return pltpu.make_async_copy(outs[a][0].at[span], outs[a][1].at[span], in_sem.at[a, i])

    ask = pltpu.make_async_copy(q_hbm, q_ref, q_sem)
    ask.start()
    for i in range(steps):
        for a in range(2):
            load(a, i).start()
    factor = math.log2(math.e) / math.sqrt(hd)
    nt = (((1,), (1,)), ((), ()))

    def query(r):
        q = q_ref[pl.ds(pl.multiple_of(r * drafts, drafts), drafts), :]
        return jnp.concatenate([q[:, h * hd : (h + 1) * hd] for h in range(heads)], axis=0)

    def weighed(r, lo, size, counts):
        k = k_ref[pl.ds(lo, size)].reshape(size * rows, hd)
        v = v_ref[pl.ds(lo, size)].reshape(size * rows, hd)
        s = lax.dot_general(query(r), k, nt, preferred_element_type=jnp.float32) * factor
        tok = tok_ref[...]
        s = [jnp.where(tok < c, s[:, x * rows : (x + 1) * rows], NEG) for x, c in enumerate(counts)]
        m = jnp.max(functools.reduce(jnp.maximum, s), axis=1, keepdims=True)
        p = [jnp.exp2(x - m) for x in s]
        mass = jnp.sum(functools.reduce(jnp.add, p), axis=1, keepdims=True)
        p = jnp.concatenate([x.astype(jnp.bfloat16) for x in p], axis=1)
        return m, mass, jnp.dot(p, v, preferred_element_type=jnp.float32)

    def merge(r, m, mass, o):
        old = top[r]
        new = jnp.maximum(old, m)
        a, b = jnp.exp2(old - new), jnp.exp2(m - new)
        top[r] = new
        den[r] = den[r] * a + mass * b
        acc[r] = acc[r] * a + o * b

    def settled(i):
        stay = dst_ref[base + i * STEP] < 0
        for b in range(1, STEP):
            stay = stay & (dst_ref[base + i * STEP + b] < 0)
        return stay

    def all_out(a, i):
        span = pl.ds(i * STEP, STEP)
        return pltpu.make_async_copy(outs[a][1].at[span], outs[a][2].at[span], out_sem.at[a, i * STEP])

    def one_out(a, s, blank):
        return pltpu.make_async_copy(zero.at[0] if blank else outs[a][1].at[s], outs[a][2].at[s], out_sem.at[a, s])

    def blank_tail(a, x):
        return pltpu.make_async_copy(zero.at[pl.ds(0, 8)], outs[a][2].at[pl.ds(blocks + x * 8, 8)], zero_sem.at[a, x])

    zero[...] = jnp.zeros_like(zero)
    for a in range(2):
        for x in range(n // 8):
            blank_tail(a, x).start()
    side = lax.broadcasted_iota(jnp.int32, tok_ref.shape, 0) // part_rows
    col = lax.broadcasted_iota(jnp.int32, tok_ref.shape, 1)
    tok_ref[...] = jnp.where(side == col % kv, col // kv, width)
    top[...] = jnp.full_like(top, NEG)
    acc[...] = jnp.zeros_like(acc)
    den[...] = jnp.zeros_like(den)
    mine = (plan_ref[...] == rank).astype(jnp.int32)
    lane = lax.broadcasted_iota(jnp.int32, plan_ref.shape, 1)
    come = jnp.zeros_like(mine)
    for x in range(hd // blocks):
        some = jnp.sum(jnp.where(lane // blocks == x, mine, 0), axis=1, keepdims=True)
        come = jnp.where(lane == x, some, come)
    arr_ref[...] = come
    ask.wait()
    line = lax.broadcasted_iota(jnp.int32, (drafts, requests), 1)
    t = lax.broadcasted_iota(jnp.int32, (drafts, kv * drafts), 0)
    u = lax.broadcasted_iota(jnp.int32, (drafts, kv * drafts), 1)

    def draft(x):
        r = rank * own + x if aligned else rank + n * x
        place = x * drafts if aligned else pl.multiple_of(r * drafts, drafts)
        dk = dk_ref[pl.ds(place, drafts), :]
        dv = dv_ref[pl.ds(place, drafts), :]
        dk = jnp.concatenate([dk[:, g * hd : (g + 1) * hd] for g in range(kv)], axis=0)
        dv = jnp.concatenate([dv[:, g * hd : (g + 1) * hd] for g in range(kv)], axis=0)
        s = lax.dot_general(query(r), dk, nt, preferred_element_type=jnp.float32) * factor
        off = jnp.sum(jnp.where(line == r, offs_ref[...], 0), axis=1, keepdims=True)
        seen = (u % drafts >= off) & (u % drafts <= t)
        bias = jnp.concatenate(
            [jnp.where(seen & (u // drafts == h // group), 0.0, NEG) for h in range(heads)], axis=0
        )
        s = jnp.where(bias < 0, NEG, s)
        m = jnp.max(s, axis=1, keepdims=True)
        p = jnp.exp2(s - m)
        top[r] = jnp.broadcast_to(m, top.shape[1:])
        den[r] = jnp.broadcast_to(jnp.sum(p, axis=1, keepdims=True), den.shape[1:])
        acc[r] = jnp.dot(p.astype(jnp.bfloat16), dv, preferred_element_type=jnp.float32)

    for x in range(own):
        if aligned:
            draft(x)
        else:
            pl.when(rank + n * x < requests)(functools.partial(draft, x))

    def step(i, _):
        calm = settled(i)
        for a in range(2):
            load(a, i).wait()

        @pl.when(calm)
        def _():
            for a in range(2):
                all_out(a, i).start()

        @pl.when(jnp.logical_not(calm))
        def _():
            for b in range(STEP):
                s = i * STEP + b
                kept = dst_ref[base + s] < 0
                for blank in (False, True):

                    @pl.when(kept != blank)
                    def _():
                        for a in range(2):
                            one_out(a, s, blank).start()

        first = i * STEP
        reqs = [req_ref[base + first + b] for b in range(STEP)]
        counts = []
        for b, r in enumerate(reqs):
            x = idx_ref[base + first + b]
            counts.append(jnp.where(x >= 0, jnp.clip(len_ref[r] - x * width, 0, width), 0))

        def alike(lo, size):
            same = jnp.bool_(True)
            for b in range(lo + 1, lo + size):
                same = same & ((reqs[b] == reqs[lo]) | (counts[b] == 0))
            return same

        def joint(lo, size):
            merge(reqs[lo], *weighed(reqs[lo], first + lo, size, counts[lo : lo + size]))

        def single(lo, size):
            some = range(lo, lo + size)
            found = [weighed(reqs[b], first + b, 1, [counts[b]]) for b in some]
            for b, parts in zip(some, found):
                merge(reqs[b], *parts)

        @pl.when(counts[0] > 0)
        def _():
            for lo in range(0, STEP, TOGETHER):
                single(lo, TOGETHER)

        return 0

    lax.fori_loop(0, steps, step, 0)
    lane = lax.broadcasted_iota(jnp.int32, (drafts, hd), 1)
    if o_ref.shape[0] > requests * drafts:
        rest = pl.ds(requests * drafts, o_ref.shape[0] - requests * drafts)
        o_ref[rest, :] = jnp.zeros_like(o_ref[rest, :])
    lse_ref[...] = jnp.full_like(lse_ref, NEG)

    def close(r, _):
        place = pl.ds(pl.multiple_of(r * drafts, drafts), drafts)
        spot = lax.rem(r, per_chunk) * LANES
        high = jnp.full((drafts, hd), NEG, jnp.float32)
        mass = jnp.ones((drafts, hd), jnp.float32)
        for h in range(heads):
            at = slice(h * drafts, (h + 1) * drafts)
            total = den[r, at, :]
            dead = total <= 0
            o = acc[r, at, :] * jnp.where(dead, 0.0, 1.0 / jnp.where(dead, 1.0, total))
            o_ref[place, h * hd : (h + 1) * hd] = o.astype(jnp.bfloat16)
            high = jnp.where(lane == spot + h, top[r, at, :], high)
            mass = jnp.where(lane == spot + h, total, mass)
        dead = mass <= 0
        level = jnp.where(dead, NEG, high + jnp.log2(jnp.where(dead, 1.0, mass)))
        line = pl.ds(pl.multiple_of(r // per_chunk * drafts, drafts), drafts)
        lse_ref[line, :] = jnp.where((lane >= spot) & (lane < spot + heads), level, lse_ref[line, :])
        return 0

    lax.fori_loop(0, requests, close, 0, unroll=4)

    def finish(i, _):
        calm = settled(i)

        @pl.when(calm)
        def _():
            for a in range(2):
                all_out(a, i).wait()

        @pl.when(jnp.logical_not(calm))
        def _():
            for b in range(STEP):
                for a in range(2):
                    one_out(a, i * STEP + b, False).wait()

        return 0

    lax.fori_loop(0, steps, finish, 0)
    for a in range(2):
        for x in range(n // 8):
            blank_tail(a, x).wait()


def attend(n, rank, tables, q_all, keys, values, dk, dv, offs, plan, kv, out_rows, aligned, own):
    blocks, rows, hd = keys.shape
    width = rows // kv
    block_req, block_idx, move_dst, lengths = tables
    drafts, requests = offs.shape
    heads = q_all.shape[1] // hd
    steps = blocks // STEP
    qrows = heads * drafts
    per_chunk = out_rows // n // drafts
    dims = (n, blocks, width, kv, heads, hd, drafts, requests, own, aligned, steps, per_chunk)
    grown = jax.ShapeDtypeStruct((blocks + n, rows, hd), keys.dtype)
    o = jax.ShapeDtypeStruct((out_rows, heads * hd), jnp.bfloat16)
    lse = jax.ShapeDtypeStruct((n * drafts, hd), jnp.float32)
    arr = jax.ShapeDtypeStruct(plan.shape, jnp.int32)
    dma = pltpu.SemaphoreType.DMA
    return pl.pallas_call(
        functools.partial(attend_kernel, dims),
        out_shape=[grown, grown, o, lse, arr],
        in_specs=[SMEM] * 5 + [ANY] * 3 + [VMEM] * 4,
        out_specs=[ANY, ANY, VMEM, VMEM, VMEM],
        scratch_shapes=[
            pltpu.VMEM(q_all.shape, q_all.dtype),
            pltpu.VMEM(keys.shape, keys.dtype),
            pltpu.VMEM(keys.shape, keys.dtype),
            pltpu.VMEM((qrows, rows), jnp.int32),
            pltpu.VMEM((requests, qrows, hd), jnp.float32),
            pltpu.VMEM((requests, qrows, hd), jnp.float32),
            pltpu.VMEM((requests, qrows, hd), jnp.float32),
            pltpu.VMEM((STEP, rows, hd), keys.dtype),
            dma,
            dma((2, steps)),
            dma((2, blocks)),
            dma((2, n // 8)),
        ],
        compiler_params=pltpu.CompilerParams(vmem_limit_bytes=60 * 1024 * 1024),
        cost_estimate=pl.CostEstimate(
            flops=4 * blocks * qrows * rows * hd, bytes_accessed=8 * blocks * rows * hd, transcendentals=0
        ),
        name="attend",
    )(rank, block_req, block_idx, move_dst, lengths, q_all, keys, values, dk, dv, offs, plan)


def merge_parts(parts, out, level_out, heads, hd):
    levels = [level for _, level in parts]
    drafts = levels[0].shape[0]
    best = functools.reduce(jnp.maximum, levels)
    weights = [jnp.exp2(x - best) for x in levels]
    mass = functools.reduce(jnp.add, weights)
    norm = 1.0 / mass
    weights = [x * norm for x in weights]
    for x in range(out.shape[0] // drafts):
        place = slice(x * drafts, (x + 1) * drafts)
        for h in range(heads):
            cols = slice(h * hd, (h + 1) * hd)
            lane = x * LANES + h
            total = None
            for (view, _), weight in zip(parts, weights):
                term = weight[:, lane : lane + 1] * view[place, cols].astype(jnp.float32)
                total = term if total is None else total + term
            out[place, cols] = total.astype(jnp.bfloat16)
    if level_out is not None:
        level_out[...] = best + jnp.log2(mass)


def combine_kernel(
    dims,
    o_ref,
    lse_ref,
    w_ref,
    far_ref,
    out_ref,
    come_ref,
    near_o,
    near_l,
    sum_o,
    sum_l,
    line_o,
    line_l,
    attn_own,
    attn,
    part,
    got,
    mix,
    *sems,
):
    n, nh, chunk, heads, hd, rows = dims
    nos, nor, nls, nlr, los, lor, lls, llr, ups, dns, zr, ps, pr, hs, hr, ms, mr, local = sems
    half = n // 2
    me = lax.axis_index("ctx")
    hme = lax.axis_index("head")
    row, side = me // 2, lax.rem(me, 2)
    partner = row * 2 + 1 - side
    greet([("ctx", n), ("head", nh)])
    low = row < half // 2
    own_turn = jnp.where(low, half - 1 - row, row)

    def turn(k):
        x = k + jnp.where(k >= own_turn, 1, 0)
        return jnp.where(low, half - 1 - x, x)

    def near(r):
        c = r * 2 + 1 - side
        return (
            remote(lse_ref.at[c], near_l.at[r], nls.at[r], nlr.at[r], "ctx", partner),
            remote(o_ref.at[c], near_o.at[r], nos.at[r], nor.at[r], "ctx", partner),
        )

    def along(r):
        to = jnp.where(r > row, row + 1, row - 1)
        slot = jnp.where((r < row) & (to == r), half, r)
        return (
            remote(sum_l.at[r], line_l.at[slot], lls.at[r], llr.at[slot], "ctx", to * 2 + side),
            remote(sum_o.at[r], line_o.at[slot], los.at[r], lor.at[slot], "ctx", to * 2 + side),
        )

    def arrived(slot):
        remote(sum_l.at[0], line_l.at[slot], lls.at[0], llr.at[slot], "ctx", partner).wait_recv()
        remote(sum_o.at[0], line_o.at[slot], los.at[0], lor.at[slot], "ctx", partner).wait_recv()

    def blank(slot):
        line_l[slot] = jnp.full(line_l.shape[1:], NEG, jnp.float32)
        line_o[slot] = jnp.zeros(line_o.shape[1:], line_o.dtype)

    for k in range(half - 1):
        for c in near(turn(k)):
            c.start()
    for c in near(row):
        c.start()

    @pl.when(row == 0)
    def _():
        for r in range(half):
            blank(r)

    @pl.when(row == half - 1)
    def _():
        for r in range(half - 1):
            blank(r)
        blank(half)

    def reduce(k, _):
        r = turn(k)
        for c in near(r):
            c.wait_recv()

        @pl.when(jnp.where(r > row, row > 0, row < half - 1))
        def _():
            arrived(r)

        at = r * 2 + side
        merge_parts(
            [(o_ref.at[at], lse_ref[at]), (near_o.at[r], near_l[r]), (line_o.at[r], line_l[r])],
            sum_o.at[r],
            sum_l.at[r],
            heads,
            hd,
        )
        for c in along(r):
            c.start()
        return 0

    lax.fori_loop(0, half - 1, reduce, 0)
    relocate(far_ref, come_ref, ms, mr, me, partner).start()
    for c in near(row):
        c.wait_recv()

    @pl.when(row > 0)
    def _():
        arrived(row)

    @pl.when(row < half - 1)
    def _():
        arrived(half)

    merge_parts(
        [
            (o_ref.at[me], lse_ref[me]),
            (near_o.at[row], near_l[row]),
            (line_o.at[row], line_l[row]),
            (line_o.at[half], line_l[half]),
        ],
        attn_own,
        None,
        heads,
        hd,
    )
    mine = pltpu.make_async_copy(attn_own, attn.at[me], local)
    mine.start()

    def upward(r):
        src = attn.at[r * 2 + side]
        return remote(src, src, ups.at[r], zr.at[r], "ctx", (row + 1) * 2 + side)

    def downward(r):
        src = attn.at[r * 2 + side]
        return remote(src, src, dns.at[r], zr.at[r], "ctx", (row - 1) * 2 + side)

    def across(r):
        src = attn.at[r * 2 + side]
        return remote(src, src, ps.at[r], pr.at[r], "ctx", partner)

    def crossed(r):
        dst = attn.at[r * 2 + 1 - side]
        remote(attn_own, dst, ps.at[r], pr.at[r], "ctx", partner).wait_recv()

    w = w_ref[...]

    def project(j):
        e = lax.rem(j + nh - hme, nh)
        value = jnp.dot(
            attn_rows(attn, pl.multiple_of(j * rows, 16), rows, chunk), w, preferred_element_type=jnp.float32
        )

        @pl.when(e == 0)
        def _():
            mix[...] = value

        @pl.when(e != 0)
        def _():
            part[e] = value.astype(jnp.bfloat16)
            remote(part.at[e], got.at[e], hs.at[e], hr.at[e], "head", j).start()

    mine.wait()
    pl.when(row < half - 1)(lambda: upward(row).start())
    pl.when(row > 0)(lambda: downward(row).start())
    across(row).start()
    matched = rows == 2 * chunk and nh == half

    def take(d):
        for r, ok, more, on in (
            (row - d, row >= d, row < half - 1, upward),
            (row + d, row + d < half, row > 0, downward),
        ):

            @pl.when(ok)
            def _():
                remote(attn_own, attn.at[r * 2 + side], ups.at[r], zr.at[r], "ctx", partner).wait_recv()
                pl.when(more)(lambda: on(r).start())
                across(r).start()

    def use(d):
        for r, ok in ((row - d, row >= d), (row + d, row + d < half)):

            @pl.when(ok)
            def _():
                crossed(r)
                project(r)

    for d in range(1, half):
        take(d)
        if d == max(half - 2, 1):
            for x in range(n):
                pl.when(row != x // 2)(lambda: relocate(far_ref, come_ref, ms, mr, me, x).start())
        if matched:
            if d == 1:
                crossed(row)
                project(row)
            else:
                use(d - 1)
    if matched:
        use(half - 1)
    else:
        for r in range(half):
            crossed(r)
        for d in range(nh):
            project(lax.rem(hme + 1 + d, nh))
    total = mix[...]
    for e in range(1, nh):
        c = remote(part.at[e], got.at[e], hs.at[e], hr.at[e], "head", lax.rem(hme + e, nh))
        c.wait_recv()
        total += got[e].astype(jnp.float32)
    out_ref[...] = total.astype(jnp.bfloat16)
    for e in range(1, nh):
        remote(part.at[e], got.at[e], hs.at[e], hr.at[e], "head", lax.rem(hme + e, nh)).wait_send()
    for k in range(half - 1):
        r = turn(k)
        for c in near(r) + along(r):
            c.wait_send()
    for c in near(row):
        c.wait_send()
    for r in range(half):
        pl.when((row < half - 1) & (r <= row))(lambda: upward(r).wait_send())
        pl.when((row > 0) & (r >= row))(lambda: downward(r).wait_send())
        across(r).wait_send()
    settle(n, far_ref, come_ref, ms, mr, me, partner)


def attn_rows(attn, start, rows, chunk):
    piece = math.gcd(rows, chunk)
    out = []
    for x in range(rows // piece):
        at = start + x * piece
        out.append(attn[at // chunk, pl.ds(pl.multiple_of(lax.rem(at, chunk), 16), piece), :])
    return jnp.concatenate(out, axis=0)


def combine(n, nh, o, lse, w, far, tokens):
    _, chunk, cols = o.shape
    drafts, hd = lse.shape[1:]
    heads = cols // hd
    rows = tokens // nh
    wide = w.shape[1]
    half = n // 2
    dims = (n, nh, chunk, heads, hd, rows)
    dma = pltpu.SemaphoreType.DMA
    outs = lambda count: pltpu.VMEM((count, chunk, cols), jnp.bfloat16)
    levels = lambda count: pltpu.VMEM((count, drafts, hd), jnp.float32)
    return pl.pallas_call(
        functools.partial(combine_kernel, dims),
        out_shape=[jax.ShapeDtypeStruct((rows, wide), jnp.bfloat16), jax.ShapeDtypeStruct(far.shape, far.dtype)],
        in_specs=[VMEM] * 3 + [ANY],
        out_specs=[VMEM, ANY],
        scratch_shapes=[outs(half), levels(half), outs(half), levels(half), outs(half + 1), levels(half + 1)]
        + [
            pltpu.VMEM((chunk, cols), jnp.bfloat16),
            pltpu.VMEM((n, chunk, cols), jnp.bfloat16),
            pltpu.VMEM((nh, rows, wide), jnp.bfloat16),
            pltpu.VMEM((nh, rows, wide), jnp.bfloat16),
            pltpu.VMEM((rows, wide), jnp.float32),
        ]
        + [dma((half,))] * 4
        + [dma((half + 1,))] * 4
        + [dma((half,))] * 5
        + [dma((nh,))] * 2
        + [dma((n,))] * 2
        + [dma],
        compiler_params=pltpu.CompilerParams(
            collective_id=1, has_side_effects=True, vmem_limit_bytes=60 * 1024 * 1024
        ),
        name="combine",
    )(o, lse, w, far)


def shards(
    n,
    nh,
    queries,
    draft_keys,
    draft_values,
    cache_keys,
    cache_values,
    w_out,
    lengths,
    block_req,
    block_idx,
    move_dst,
    draft_offs,
):
    blocks, width, kv, hd = cache_keys.shape
    requests, drafts = draft_offs.shape
    tokens = requests * drafts
    local_tokens = queries.shape[0]
    heads = queries.shape[1] // hd
    me = lax.axis_index("ctx")
    rank = jnp.reshape(me, (1,)).astype(jnp.int32)
    keys = cache_keys.reshape(blocks, width * kv, hd)
    values = cache_values.reshape(blocks, width * kv, hd)
    early, big, small = pack(n, rank, move_dst, keys, values)

    aligned = local_tokens % drafts == 0
    if aligned:
        own = local_tokens // drafts
        q_all, early = gather_all(n, [queries], early)
        dk, dv = draft_keys, draft_values
    else:
        own = -(-requests // n)
        q_all, dk, dv, early = gather_all(n, [queries, draft_keys, draft_values], early)
        dk, dv = dk.reshape(tokens, -1), dv.reshape(tokens, -1)
    big, q_all = lax.optimization_barrier((big, q_all))
    big = lax.all_to_all(big, "ctx", split_axis=0, concat_axis=0, tiled=True)
    q_all = q_all.reshape(tokens, heads * hd)
    chunk = -(-requests // n) * drafts
    new_keys, new_values, o, lse, arriving = attend(
        n,
        rank,
        (block_req, block_idx, move_dst, lengths),
        q_all,
        keys,
        values,
        dk,
        dv,
        draft_offs.T,
        move_dst.reshape(-1, hd),
        kv,
        n * chunk,
        aligned,
        own,
    )
    mixed, small = combine(n, nh, o.reshape(n, chunk, -1), lse.reshape(n, drafts, hd), w_out, small, tokens)
    new_keys, new_values = unpack(n, blocks, arriving, (early, big, small), new_keys, new_values)
    shape = (blocks + n, width, kv, hd)
    return (mixed, new_keys.reshape(shape), new_values.reshape(shape))


def solution(mesh):
    in_specs = (
        P("ctx", "head"),
        P("ctx", "head"),
        P("ctx", "head"),
        P("ctx", None, "head", None),
        P("ctx", None, "head", None),
        P("head", "ctx"),
        P(),
        P(),
        P(),
        P(),
        P(),
    )
    out_specs = (P("head", "ctx"), P("ctx", None, "head", None), P("ctx", None, "head", None))
    body = functools.partial(shards, mesh.shape["ctx"], mesh.shape["head"])
    return jax.shard_map(body, mesh=mesh, in_specs=in_specs, out_specs=out_specs, check_vma=False)
```
